32 devices in a mesh: groups: 2 (over x), rows: 4 (over y, core), cols: 4 (over z).
Axes of the slice: x: 2, y: 2, z: 4, core: 2. Of those that a mesh axis runs over, the one named last changes fastest.
Arguments:
- tokens: bfloat16 [128, 32, 512], P(('groups', 'rows'), 'cols'), parts along dimension 0, may hold values from -6 to 6
- top_state: bfloat16 [64, 16, 2048], P(('groups', 'cols')), parts along dimension 0, may hold values from -4 to 4
- in_weight: bfloat16 [512, 1024], replicated, may hold values from -0.25 to 0.25
- conv_weight: float32 [9, 512], replicated, may hold values from -2 to 2
- bc_weight: bfloat16 [512, 256], replicated, may hold values from -0.25 to 0.25
- step_weight: bfloat16 [512, 32], replicated, may hold values from -0.25 to 0.25
- step_bias: float32 [32], replicated, may hold values from -2 to 0.5
- across_rate: float32 [16], replicated, may hold values from 0.03125 to 0.3
- down_rate: float32 [16], replicated, may hold values from 0.015625 to 0.3
- skip_gain: float32 [16], replicated, may hold values from 0.5 to 1.5
- norm_gain: float32 [512], replicated, may hold values from 0.1 to 1.9
- out_weight: bfloat16 [512, 512], replicated, may hold values from -0.25 to 0.25
Outputs:
- layer_out: bfloat16 [128, 32, 512], P(('groups', 'rows'), 'cols'), parts along dimension 0
The draws below stay inside these ranges and needn't reach their ends.
There are 2 independent parts, one for each index of `groups`. The reference program is written for one: setup_inputs(seed, part) draws one part's arguments, and reference() takes and returns one part's arrays. A program takes and returns all parts, laid end to end along the dimension named above; an argument that names none is the same for every part. Nothing has to cross between parts.
All inputs are finite; a program needn't handle non-finite values.
Results may differ from the reference program's by a relative error of at most 0.0095.
Values may be sent and summed in bfloat16 or wider, within the bound.
A program may use at most 128 MiB of HBM per device.

```python
import math
import jax
import jax.numpy as jnp
from jax import lax

D = 512
HEADS = 16
HEAD_DIM = 32
STATE = 64
INNER = 512
HEIGHT = 64
WIDTH = 32


def block_levels(stream_key, extent, shards, least, high):
    gain = 1.0
    for axis_at, parts in shards:
        draws = jax.random.uniform(jax.random.fold_in(jax.random.fold_in(stream_key, 6), axis_at), (parts,), jnp.float32, least / len(shards), high / len(shards))
        gain = gain * jnp.repeat(jnp.exp(draws), extent[axis_at] // parts).reshape((-1,) + (1,) * (len(extent) - 1 - axis_at))
    return gain


def gaussian(stream_key, dims, deviation, bound, cuts=(), held_as=jnp.bfloat16):
    values = deviation * jax.random.normal(stream_key, dims, jnp.float32)
    if cuts:
        values = values * block_levels(stream_key, dims, cuts, -0.22, 0.18)
    return jnp.clip(values, -bound, bound).astype(held_as)


def setup_inputs(seed: int = 0, part: int = 0) -> dict:
    splits = jax.random.split(jax.random.key(seed), 13)
    part_keys = jax.random.split(jax.random.fold_in(splits[12], part), 13)
    tokens = gaussian(part_keys[0], (HEIGHT, WIDTH, D), 1.0, 6.0, ((0, 4), (1, 4)))
    top_state = gaussian(part_keys[1], (WIDTH, HEADS, HEAD_DIM * STATE), 0.3, 4.0, ((0, 4),))
    in_weight = gaussian(splits[2], (D, 2 * INNER), D ** -0.5, 0.25)
    conv_weight = gaussian(splits[3], (9, INNER), 9 ** -0.5, 2.0, (), jnp.float32)
    bc_weight = gaussian(splits[4], (INNER, 4 * STATE), INNER ** -0.5, 0.25)
    step_weight = gaussian(splits[5], (INNER, 2 * HEADS), INNER ** -0.5, 0.25)
    step_bias = jnp.clip(jax.random.uniform(splits[6], (2 * HEADS,), jnp.float32, -2.0, 0.5), -2.0, 0.5)
    across_rate = jnp.clip(jnp.exp(jax.random.uniform(splits[7], (HEADS,), jnp.float32, math.log(0.03125), math.log(0.3))), 0.03125, 0.3)
    down_rate = jnp.clip(jnp.exp(jax.random.uniform(splits[8], (HEADS,), jnp.float32, math.log(0.015625), math.log(0.3))), 0.015625, 0.3)
    skip_gain = jnp.clip(jax.random.uniform(splits[9], (HEADS,), jnp.float32, 0.5, 1.5), 0.5, 1.5)
    norm_gain = jnp.clip(1.0 + 0.18 * jax.random.normal(splits[10], (INNER,), jnp.float32), 0.1, 1.9)
    out_weight = gaussian(splits[11], (INNER, D), INNER ** -0.5, 0.25)
    return dict(tokens=tokens, top_state=top_state, in_weight=in_weight, conv_weight=conv_weight, bc_weight=bc_weight, step_weight=step_weight, step_bias=step_bias, across_rate=across_rate, down_rate=down_rate, skip_gain=skip_gain, norm_gain=norm_gain, out_weight=out_weight)


def sweep(decay, steps, values, b_in, c_in, start):

    def advance(state, items):
        rate, size, entry, b_row, c_row = items
        state = rate[..., None, None] * state + (size[..., None] * entry)[..., None] * b_row[:, None, None, :]
        emitted = jnp.einsum('akpn,an->akp', state, c_row, precision=lax.Precision.HIGHEST)
        return (state, emitted)
    final, emitted = lax.scan(advance, start, (decay, steps, values, b_in, c_in))
    return emitted

def reference(tokens, top_state, in_weight, conv_weight, bc_weight, step_weight, step_bias, across_rate, down_rate, skip_gain, norm_gain, out_weight):
    height = tokens.shape[0]
    width = tokens.shape[1]
    projected = jnp.dot(tokens.reshape(-1, D), in_weight, preferred_element_type=jnp.float32).reshape(height, width, 2 * INNER)
    mixer_in = projected[..., :INNER].astype(jnp.bfloat16)
    gate_in = projected[..., INNER:].astype(jnp.bfloat16)
    padded = jnp.pad(mixer_in.astype(jnp.float32), ((1, 1), (1, 1), (0, 0)))
    summed = jnp.zeros((height, width, INNER), jnp.float32)
    for row_off in range(3):
        for col_off in range(3):
            summed = summed + conv_weight[3 * row_off + col_off] * padded[row_off:row_off + height, col_off:col_off + width]
    values_low = jax.nn.silu(summed).astype(jnp.bfloat16)
    flat = values_low.reshape(-1, INNER)
    maps = jnp.dot(flat, bc_weight, preferred_element_type=jnp.float32).reshape(height, width, 4 * STATE)
    steps = jax.nn.softplus(jnp.dot(flat, step_weight, preferred_element_type=jnp.float32) + step_bias).reshape(height, width, 2 * HEADS)
    values = values_low.astype(jnp.float32).reshape(height, width, HEADS, HEAD_DIM)
    step_across = steps[..., :HEADS]
    step_down = steps[..., HEADS:]
    decay_across = jnp.exp(-step_across * across_rate)
    decay_down = jnp.exp(-step_down * down_rate)
    b_across = maps[..., :STATE]
    c_across = maps[..., STATE:2 * STATE]
    b_down = maps[..., 2 * STATE:3 * STATE]
    c_down = maps[..., 3 * STATE:]
    moved = [jnp.moveaxis(item, 1, 0) for item in (decay_across, step_across, values, b_across, c_across)]
    start_across = jnp.zeros((height, HEADS, HEAD_DIM, STATE), jnp.float32)
    y_across = jnp.moveaxis(sweep(moved[0], moved[1], moved[2], moved[3], moved[4], start_across), 0, 1)
    start_down = top_state.astype(jnp.float32).reshape(width, HEADS, HEAD_DIM, STATE)
    y_down = sweep(decay_down, step_down, values, b_down, c_down, start_down)
    mixed = y_across + y_down + skip_gain[:, None] * values
    gated = mixed.reshape(height, width, INNER) * jax.nn.silu(gate_in.astype(jnp.float32))
    scale = lax.rsqrt(lax.optimization_barrier(jnp.mean(gated * gated, axis=-1, keepdims=True)) + 1e-05)
    normed = (gated * scale * norm_gain).astype(jnp.bfloat16)
    result = jnp.dot(normed.reshape(-1, INNER), out_weight, preferred_element_type=jnp.float32)
    return result.astype(jnp.bfloat16).reshape(height, width, D)
```

```python
import functools

import jax
import jax.numpy as jnp
from jax import lax
from jax.experimental import pallas as pl
from jax.experimental.pallas import tpu as pltpu
from jax.sharding import PartitionSpec as P

F32 = jnp.float32
BF16 = jnp.bfloat16
NEIGHBOURS = ((-1, 0), (1, 0), (0, -1), (0, 1), (-1, -1), (-1, 1), (1, -1), (1, 1))
OPPOSITE = (1, 0, 3, 2, 7, 6, 5, 4)
STRIP = 16
LANES = 128


def dot(a, b):
    return jnp.dot(a, b, preferred_element_type=F32)


def dot_nt(a, b):
    return lax.dot_general(a, b, (((1,), (1,)), ((), ())), preferred_element_type=F32)


def split_dot(mask, x):
    high = x.astype(BF16)
    rest = x - high.astype(F32)
    middle = rest.astype(BF16)
    low = (rest - middle.astype(F32)).astype(BF16)
    return dot(mask, high) + dot(mask, middle) + dot(mask, low)


def expand(x, spread):
    high = x.astype(BF16)
    low = (x - high.astype(F32)).astype(BF16)
    return dot(high, spread) + dot(low, spread)


def softplus(x):
    return jnp.maximum(x, 0.0) + jnp.log1p(jnp.exp(-jnp.abs(x)))


def silu(x):
    return x / (1.0 + jnp.exp(-x))


def kernel(
    nr, nc, R, C, heads,
    tok, top, win, wm, wout, small, out,
    edge, halo, halo_f, pad, gate, vals, rva, rvd, acc, weighted, y_ref,
    hs_sem, hr_sem, as_sem, ar_sem, ds_sem, dr_sem,
):
    count = R * C
    inner = wout.shape[0]
    state = (wm.shape[1] - LANES) // 4
    width = inner // heads
    i = lax.axis_index("rows")
    j = lax.axis_index("cols")
    mesh = pl.DeviceIdType.MESH

    def exists(k):
        di, dj = NEIGHBOURS[k]
        a, b = i + di, j + dj
        return (a >= 0) & (a < nr) & (b >= 0) & (b < nc)

    def target(k):
        di, dj = NEIGHBOURS[k]
        return {"rows": i + di, "cols": j + dj}

    barrier = pltpu.get_barrier_semaphore()
    for d in range(1, nc):
        pl.semaphore_signal(
            barrier, inc=1, device_id={"cols": lax.rem(j + d, nc)}, device_id_type=mesh
        )
    for d in range(1, nr):
        pl.semaphore_signal(
            barrier, inc=1, device_id={"rows": lax.rem(i + d, nr)}, device_id_type=mesh
        )
    for k in range(4, 8):
        @pl.when(exists(k))
        def _(k=k):
            pl.semaphore_signal(barrier, inc=1, device_id=target(k), device_id_type=mesh)

    pos = lax.broadcasted_iota(jnp.int32, (2 * R, count), 0)
    src = lax.broadcasted_iota(jnp.int32, (2 * R, count), 1)
    wanted = jnp.where(pos < R, pos * C, (pos - R) * C + C - 1)
    edge[...] = dot((src == wanted).astype(F32).astype(BF16), tok[...]).astype(BF16)
    corners = sum(jnp.where(exists(k), 1, 0) for k in range(4, 8))
    pl.semaphore_wait(barrier, nc - 1 + nr - 1 + corners)

    def halo_copy(k):
        di, dj = NEIGHBOURS[k]
        if di < 0:
            piece = tok.at[pl.ds(0, STRIP)]
        elif di > 0:
            piece = tok.at[pl.ds(count - STRIP, STRIP)]
        else:
            piece = edge.at[pl.ds(0 if dj < 0 else R, STRIP)]
        return pltpu.make_async_remote_copy(
            src_ref=piece,
            dst_ref=halo.at[pl.ds(OPPOSITE[k] * STRIP, STRIP)],
            send_sem=hs_sem.at[k],
            recv_sem=hr_sem.at[OPPOSITE[k]],
            device_id=target(k),
            device_id_type=mesh,
        )

    for k in range(8):
        @pl.when(exists(k))
        def _(k=k):
            halo_copy(k).start()

        @pl.when(jnp.logical_not(exists(k)))
        def _(k=k):
            halo[pl.ds(k * STRIP, STRIP)] = jnp.zeros((STRIP, halo.shape[1]), BF16)

    projected = dot(tok[...], win[...])
    gate[...] = silu(projected[:, inner:].astype(BF16).astype(F32))
    mixer = projected[:, :inner].astype(BF16).astype(F32)
    pad[pl.ds(1, R), pl.ds(8, C), :] = mixer.reshape(R, C, inner)

    for k in range(8):
        @pl.when(exists(k))
        def _(k=k):
            pltpu.make_async_remote_copy(
                src_ref=edge.at[pl.ds(0, STRIP)],
                dst_ref=halo.at[pl.ds(k * STRIP, STRIP)],
                send_sem=hs_sem.at[k],
                recv_sem=hr_sem.at[k],
                device_id=target(k),
                device_id_type=mesh,
            ).wait_recv()

    halo_f[...] = dot(halo[...], win[:, :inner]).astype(BF16).astype(F32)

    def halo_rows(k, first, n):
        return halo_f[pl.ds(k * STRIP + first, n), :]

    pad[0, pl.ds(8, C), :] = halo_rows(0, STRIP - C, C)
    pad[R + 1, pl.ds(8, C), :] = halo_rows(1, 0, C)
    for r in range(R):
        pad[1 + r, pl.ds(7, 1), :] = halo_rows(2, r, 1)
        pad[1 + r, pl.ds(8 + C, 1), :] = halo_rows(3, r, 1)
    pad[0, pl.ds(7, 1), :] = halo_rows(4, STRIP - 1, 1)
    pad[0, pl.ds(8 + C, 1), :] = halo_rows(5, STRIP - C, 1)
    pad[R + 1, pl.ds(7, 1), :] = halo_rows(6, C - 1, 1)
    pad[R + 1, pl.ds(8 + C, 1), :] = halo_rows(7, 0, 1)

    summed = jnp.zeros((R, C, inner), F32)
    for b in range(3):
        moved = pad[:, pl.ds(7 + b, C), :]
        for a in range(3):
            tap = small[pl.ds(3 * a + b, 1), :].reshape(1, 1, inner)
            summed = summed + tap * moved[a : a + R]
    values_f = silu(summed).reshape(count, inner).astype(BF16).astype(F32)
    vals[...] = values_f.astype(BF16)

    def send_a(d):
        return pltpu.make_async_remote_copy(
            src_ref=vals,
            dst_ref=rva.at[j],
            send_sem=as_sem.at[d],
            recv_sem=ar_sem.at[j],
            device_id={"cols": j + d},
            device_id_type=mesh,
        )

    def send_d(d):
        return pltpu.make_async_remote_copy(
            src_ref=vals,
            dst_ref=rvd.at[i],
            send_sem=ds_sem.at[d],
            recv_sem=dr_sem.at[i],
            device_id={"rows": i + d},
            device_id_type=mesh,
        )

    for d in range(1, max(nc, nr)):
        if d < nc:
            @pl.when(j + d < nc)
            def _(d=d):
                send_a(d).start()
        if d < nr:
            @pl.when(i + d < nr)
            def _(d=d):
                send_d(d).start()

    q = lax.broadcasted_iota(jnp.int32, (count, count), 0)
    k_ = lax.broadcasted_iota(jnp.int32, (count, count), 1)
    same_row = lax.div(q, C) == lax.div(k_, C)
    same_col = lax.rem(q, C) == lax.rem(k_, C)
    upto = k_ <= q
    after = k_ > q

    def as_mask(m):
        return jnp.where(m, 1.0, 0.0).astype(BF16)

    lane = lax.broadcasted_iota(jnp.int32, (count, LANES), 1)
    spot = lax.broadcasted_iota(jnp.int32, (LANES, inner), 0)
    head = lax.div(lax.broadcasted_iota(jnp.int32, (LANES, inner), 1), width)
    spread_a = as_mask(spot == head)
    spread_d = as_mask(spot == head + heads)
    bias = small[pl.ds(11, 1), :LANES]
    rate = small[pl.ds(12, 1), :LANES]

    maps = dot(vals[...], wm[...])
    steps = softplus(maps[:, 4 * state :] + bias)
    log_decay = -steps * rate
    cum_a = split_dot(as_mask(same_row & upto), log_decay)
    cum_d = split_dot(as_mask(same_col & upto), log_decay)
    map_a = maps[:, : 2 * state]
    map_d = maps[:, 2 * state : 4 * state]
    c_a = jnp.where(lane < state, pltpu.roll(map_a, state, 1), 0.0).astype(BF16)
    c_d = jnp.where(lane < state, pltpu.roll(map_d, state, 1), 0.0).astype(BF16)
    score_a = jnp.where(same_row & upto, dot_nt(c_a, map_a.astype(BF16)), 0.0)
    score_d = jnp.where(same_col & upto, dot_nt(c_d, map_d.astype(BF16)), 0.0)
    weighted[pl.ds(0, count), :] = (values_f * expand(steps, spread_a)).astype(BF16)
    weighted[pl.ds(count, count), :] = (values_f * expand(steps, spread_d)).astype(BF16)
    cum_at = cum_a.T
    cum_dt = cum_d.T
    per_group = LANES // width
    for g in range(inner // LANES):
        total = jnp.zeros((count, LANES), F32)
        for e in range(per_group):
            h = g * per_group + e
            diff_a = cum_a[:, h : h + 1] - cum_at[h : h + 1, :]
            hd = heads + h
            diff_d = cum_d[:, hd : hd + 1] - cum_dt[hd : hd + 1, :]
            mix_a = (jnp.exp(jnp.minimum(diff_a, 0.0)) * score_a).astype(BF16)
            mix_d = (jnp.exp(jnp.minimum(diff_d, 0.0)) * score_d).astype(BF16)
            mix = jnp.concatenate([mix_a, mix_d], axis=1)
            part = dot(mix, weighted[:, g * LANES : (g + 1) * LANES])
            total = jnp.where(lax.div(lane, width) == e, part, total)
        y_ref[:, g * LANES : (g + 1) * LANES] = total

    column = lax.rem(lax.broadcasted_iota(jnp.int32, (count, state), 0), C)
    c_top = c_d[:, :state].astype(F32)
    from_top = jnp.zeros((count, inner), F32)
    for c in range(C):
        rows = jnp.where(column == c, c_top, 0.0).astype(BF16)
        from_top = from_top + dot_nt(rows, top[pl.ds(c * inner, inner), :])

    def remote(buffer, slot, c_map, first, same, spread, gap):
        block = buffer[slot]
        m = dot(block, wm[:, first : first + 2 * state]).astype(BF16)
        s = softplus(dot(block, wm[:, 4 * state :]) + bias)
        ld = -s * rate
        tail = split_dot(as_mask(same & after), ld)
        whole = split_dot(as_mask(same), ld)
        weight = s * jnp.exp(tail + gap)
        entry = (block.astype(F32) * expand(weight, spread)).astype(BF16)
        score = jnp.where(same, dot_nt(c_map, m), 0.0).astype(BF16)
        acc[...] += dot(score, entry)
        return gap + whole

    acc[...] = jnp.zeros_like(acc)

    def hop_a(t, gap):
        slot = j - 1 - t
        pltpu.make_async_remote_copy(
            src_ref=vals, dst_ref=rva.at[slot], send_sem=as_sem.at[0],
            recv_sem=ar_sem.at[slot], device_id={"cols": slot}, device_id_type=mesh,
        ).wait_recv()
        return remote(rva, slot, c_a, 0, same_row, spread_a, gap)

    lax.fori_loop(0, j, hop_a, jnp.zeros((count, LANES), F32))
    y_ref[...] += expand(jnp.exp(cum_a), spread_a) * acc[...]
    acc[...] = jnp.zeros_like(acc)

    def hop_d(t, gap):
        slot = i - 1 - t
        pltpu.make_async_remote_copy(
            src_ref=vals, dst_ref=rvd.at[slot], send_sem=ds_sem.at[0],
            recv_sem=dr_sem.at[slot], device_id={"rows": slot}, device_id_type=mesh,
        ).wait_recv()
        return remote(rvd, slot, c_d, 2 * state, same_col, spread_d, gap)

    gap_d = lax.fori_loop(0, i, hop_d, jnp.zeros((count, LANES), F32))
    y = (
        y_ref[...]
        + expand(jnp.exp(cum_d), spread_d) * acc[...]
        + expand(jnp.exp(cum_d + gap_d), spread_d) * from_top
        + small[pl.ds(10, 1), :] * vals[...].astype(F32)
    )
    gated = y * gate[...]
    scale = lax.rsqrt(jnp.mean(gated * gated, axis=-1, keepdims=True) + 1e-05)
    normed = (gated * scale * small[pl.ds(9, 1), :]).astype(BF16)
    out[...] = dot(normed, wout[...]).astype(BF16)

    for k in range(8):
        @pl.when(exists(k))
        def _(k=k):
            halo_copy(k).wait_send()
    for d in range(1, nc):
        @pl.when(j + d < nc)
        def _(d=d):
            send_a(d).wait_send()
    for d in range(1, nr):
        @pl.when(i + d < nr)
        def _(d=d):
            send_d(d).wait_send()


def shards(
    nr, nc,
    tokens, top_state, in_weight, conv_weight, bc_weight, step_weight, step_bias,
    across_rate, down_rate, skip_gain, norm_gain, out_weight,
):
    R, C, model = tokens.shape
    inner = out_weight.shape[0]
    heads = across_rate.shape[0]
    state = bc_weight.shape[1] // 4
    count = R * C
    wm = jnp.pad(
        jnp.concatenate([bc_weight, step_weight], axis=1), ((0, 0), (0, LANES - 2 * heads))
    )

    def row(x):
        return jnp.pad(x, (0, inner - x.shape[0]))[None]

    small = jnp.concatenate(
        [
            conv_weight,
            norm_gain[None],
            jnp.repeat(skip_gain, inner // heads)[None],
            row(step_bias),
            row(jnp.concatenate([across_rate, down_rate])),
            jnp.zeros((3, inner), F32),
        ],
        axis=0,
    )
    vmem = pl.BlockSpec(memory_space=pltpu.VMEM)
    result = pl.pallas_call(
        functools.partial(kernel, nr, nc, R, C, heads),
        out_shape=jax.ShapeDtypeStruct((count, model), BF16),
        in_specs=[vmem] * 6,
        out_specs=vmem,
        scratch_shapes=[
            pltpu.VMEM((2 * R, model), BF16),
            pltpu.VMEM((8 * STRIP, model), BF16),
            pltpu.VMEM((8 * STRIP, inner), F32),
            pltpu.VMEM((R + 2, 24, inner), F32),
            pltpu.VMEM((count, inner), F32),
            pltpu.VMEM((count, inner), BF16),
            pltpu.VMEM((nc, count, inner), BF16),
            pltpu.VMEM((nr, count, inner), BF16),
            pltpu.VMEM((count, inner), F32),
            pltpu.VMEM((2 * count, inner), BF16),
            pltpu.VMEM((count, inner), F32),
            pltpu.SemaphoreType.DMA((8,)),
            pltpu.SemaphoreType.DMA((8,)),
            pltpu.SemaphoreType.DMA((nc,)),
            pltpu.SemaphoreType.DMA((nc,)),
            pltpu.SemaphoreType.DMA((nr,)),
            pltpu.SemaphoreType.DMA((nr,)),
        ],
        compiler_params=pltpu.CompilerParams(
            collective_id=0, has_side_effects=True, vmem_limit_bytes=40 * 1024 * 1024
        ),
    )(
        tokens.reshape(count, model),
        top_state.reshape(C * inner, state),
        in_weight,
        wm,
        out_weight,
        small,
    )
    return result.reshape(R, C, model)


def solution(mesh):
    in_specs = (
        P(("groups", "rows"), "cols", None),
        P(("groups", "cols"), None, None),
    ) + (P(),) * 10
    out_specs = P(("groups", "rows"), "cols", None)
    return jax.shard_map(
        functools.partial(shards, mesh.shape["rows"], mesh.shape["cols"]),
        mesh=mesh, in_specs=in_specs, out_specs=out_specs, check_vma=False,
    )
```

```python
import functools

import jax
import jax.numpy as jnp
from jax import lax
from jax.experimental import pallas as pl
from jax.experimental.pallas import tpu as pltpu
from jax.sharding import PartitionSpec as P

F32 = jnp.float32
BF16 = jnp.bfloat16
NEIGHBOURS = ((-1, 0), (1, 0), (0, -1), (0, 1), (-1, -1), (-1, 1), (1, -1), (1, 1))
OPPOSITE = (1, 0, 3, 2, 7, 6, 5, 4)
STRIP = 16
LANES = 128


def dot(a, b):
    return jnp.dot(a, b, preferred_element_type=F32)


def dot_nt(a, b):
    return lax.dot_general(a, b, (((1,), (1,)), ((), ())), preferred_element_type=F32)


def split_dot(mask, x):
    high = x.astype(BF16)
    rest = x - high.astype(F32)
    middle = rest.astype(BF16)
    low = (rest - middle.astype(F32)).astype(BF16)
    return dot(mask, high) + dot(mask, middle) + dot(mask, low)


def split_sum(x, mask):
    high = x.astype(BF16)
    rest = x - high.astype(F32)
    middle = rest.astype(BF16)
    low = (rest - middle.astype(F32)).astype(BF16)
    return dot(high, mask) + dot(middle, mask) + dot(low, mask)


def expand(x, spread):
    high = x.astype(BF16)
    low = (x - high.astype(F32)).astype(BF16)
    return dot(high, spread) + dot(low, spread)


def softplus(x):
    return jnp.maximum(x, 0.0) + jnp.log1p(jnp.exp(-jnp.abs(x)))


def silu(x):
    return x / (1.0 + jnp.exp(-x))


def kernel(
    nr, nc, R, C, heads,
    tok_h, top_h, win_h, wbc_h, wout_h, conv, wst_t, step_bias, rate_a, rate_d, skip, gain, out,
    tok, top, win, wbc, wout, wst, param, edge, halo, halo_f, pad, gate, vals, rva, rvd, acc, weighted, y_ref,
    ld_sem, hs_sem, hr_sem, as_sem, ar_sem, ds_sem, dr_sem,
):
    count = R * C
    inner = wout.shape[0]
    state = wbc.shape[1] // 4
    width = inner // heads
    i = lax.axis_index("rows")
    j = lax.axis_index("cols")
    mesh = pl.DeviceIdType.MESH

    def exists(k):
        di, dj = NEIGHBOURS[k]
        a, b = i + di, j + dj
        return (a >= 0) & (a < nr) & (b >= 0) & (b < nc)

    def target(k):
        di, dj = NEIGHBOURS[k]
        return {"rows": i + di, "cols": j + dj}

    loads = [
        pltpu.make_async_copy(a, b, ld_sem.at[n])
        for n, (a, b) in enumerate(
            ((tok_h, tok), (win_h, win), (wbc_h, wbc), (top_h, top), (wout_h, wout))
        )
    ]
    for load in loads:
        load.start()

    barrier = pltpu.get_barrier_semaphore()
    for d in range(1, nc):
        pl.semaphore_signal(
            barrier, inc=1, device_id={"cols": lax.rem(j + d, nc)}, device_id_type=mesh
        )
    for d in range(1, nr):
        pl.semaphore_signal(
            barrier, inc=1, device_id={"rows": lax.rem(i + d, nr)}, device_id_type=mesh
        )
    for k in range(4, 8):
        @pl.when(exists(k))
        def _(k=k):
            pl.semaphore_signal(barrier, inc=1, device_id=target(k), device_id_type=mesh)

    pos = lax.broadcasted_iota(jnp.int32, (2 * R, count), 0)
    src = lax.broadcasted_iota(jnp.int32, (2 * R, count), 1)
    wanted = jnp.where(pos < R, pos * C, (pos - R) * C + C - 1)
    wst[...] = jnp.zeros_like(wst)
    wst[pl.ds(0, 2 * heads), :] = wst_t[...]
    param[...] = jnp.zeros_like(param)
    param[0:1, 0 : 2 * heads] = step_bias[...]
    param[1:2, 0:heads] = rate_a[...]
    param[1:2, heads : 2 * heads] = rate_d[...]
    param[2:3, 0:heads] = skip[...]
    loads[0].wait()
    edge[...] = dot((src == wanted).astype(F32).astype(BF16), tok[...]).astype(BF16)
    corners = sum(jnp.where(exists(k), 1, 0) for k in range(4, 8))
    pl.semaphore_wait(barrier, nc - 1 + nr - 1 + corners)

    def halo_copy(k):
        di, dj = NEIGHBOURS[k]
        if di < 0:
            piece = tok.at[pl.ds(0, STRIP)]
        elif di > 0:
            piece = tok.at[pl.ds(count - STRIP, STRIP)]
        else:
            piece = edge.at[pl.ds(0 if dj < 0 else R, STRIP)]
        return pltpu.make_async_remote_copy(
            src_ref=piece,
            dst_ref=halo.at[pl.ds(OPPOSITE[k] * STRIP, STRIP)],
            send_sem=hs_sem.at[k],
            recv_sem=hr_sem.at[OPPOSITE[k]],
            device_id=target(k),
            device_id_type=mesh,
        )

    for k in range(8):
        @pl.when(exists(k))
        def _(k=k):
            halo_copy(k).start()

        @pl.when(jnp.logical_not(exists(k)))
        def _(k=k):
            halo[pl.ds(k * STRIP, STRIP)] = jnp.zeros((STRIP, halo.shape[1]), BF16)

    loads[1].wait()
    projected = dot(tok[...], win[...])
    gate[...] = silu(projected[:, inner:].astype(BF16).astype(F32))
    mixer = projected[:, :inner].astype(BF16).astype(F32)
    pad[pl.ds(1, R), pl.ds(8, C), :] = mixer.reshape(R, C, inner)

    for k in range(8):
        @pl.when(exists(k))
        def _(k=k):
            pltpu.make_async_remote_copy(
                src_ref=edge.at[pl.ds(0, STRIP)],
                dst_ref=halo.at[pl.ds(k * STRIP, STRIP)],
                send_sem=hs_sem.at[k],
                recv_sem=hr_sem.at[k],
                device_id=target(k),
                device_id_type=mesh,
            ).wait_recv()

    halo_f[...] = dot(halo[...], win[:, :inner]).astype(BF16).astype(F32)

    def halo_rows(k, first, n):
        return halo_f[pl.ds(k * STRIP + first, n), :]

    pad[0, pl.ds(8, C), :] = halo_rows(0, STRIP - C, C)
    pad[R + 1, pl.ds(8, C), :] = halo_rows(1, 0, C)
    for r in range(R):
        pad[1 + r, pl.ds(7, 1), :] = halo_rows(2, r, 1)
        pad[1 + r, pl.ds(8 + C, 1), :] = halo_rows(3, r, 1)
    pad[0, pl.ds(7, 1), :] = halo_rows(4, STRIP - 1, 1)
    pad[0, pl.ds(8 + C, 1), :] = halo_rows(5, STRIP - C, 1)
    pad[R + 1, pl.ds(7, 1), :] = halo_rows(6, C - 1, 1)
    pad[R + 1, pl.ds(8 + C, 1), :] = halo_rows(7, 0, 1)

    summed = jnp.zeros((R, C, inner), F32)
    for b in range(3):
        moved = pad[:, pl.ds(7 + b, C), :]
        for a in range(3):
            tap = conv[pl.ds(3 * a + b, 1), :].reshape(1, 1, inner)
            summed = summed + tap * moved[a : a + R]
    values_f = silu(summed).reshape(count, inner).astype(BF16).astype(F32)
    vals[...] = values_f.astype(BF16)

    def send_a(d):
        return pltpu.make_async_remote_copy(
            src_ref=vals,
            dst_ref=rva.at[j],
            send_sem=as_sem.at[d],
            recv_sem=ar_sem.at[j],
            device_id={"cols": j + d},
            device_id_type=mesh,
        )

    def send_d(d):
        return pltpu.make_async_remote_copy(
            src_ref=vals,
            dst_ref=rvd.at[i],
            send_sem=ds_sem.at[d],
            recv_sem=dr_sem.at[i],
            device_id={"rows": i + d},
            device_id_type=mesh,
        )

    for d in range(1, max(nc, nr)):
        if d < nc:
            @pl.when(j + d < nc)
            def _(d=d):
                send_a(d).start()
        if d < nr:
            @pl.when(i + d < nr)
            def _(d=d):
                send_d(d).start()

    q = lax.broadcasted_iota(jnp.int32, (count, count), 0)
    k_ = lax.broadcasted_iota(jnp.int32, (count, count), 1)
    same_row = lax.div(q, C) == lax.div(k_, C)
    same_col = lax.rem(q, C) == lax.rem(k_, C)
    upto = k_ <= q
    after = k_ > q

    def as_mask(m):
        return jnp.where(m, 1.0, 0.0).astype(BF16)

    lane = lax.broadcasted_iota(jnp.int32, (count, LANES), 1)
    spot = lax.broadcasted_iota(jnp.int32, (LANES, inner), 0)
    head = lax.div(lax.broadcasted_iota(jnp.int32, (LANES, inner), 1), width)
    spread_a = as_mask(spot == head)
    spread_d = as_mask(spot == head + heads)
    bias = param[0:1, :]
    rate = param[1:2, :]

    loads[2].wait()
    maps = dot(vals[...], wbc[...])
    steps = softplus(dot_nt(vals[...], wst[...]) + bias)
    log_decay = -steps * rate
    cum_a = split_dot(as_mask(same_row & upto), log_decay)
    cum_d = split_dot(as_mask(same_col & upto), log_decay)
    map_a = maps[:, : 2 * state]
    map_d = maps[:, 2 * state : 4 * state]
    c_a = jnp.where(lane < state, pltpu.roll(map_a, state, 1), 0.0).astype(BF16)
    c_d = jnp.where(lane < state, pltpu.roll(map_d, state, 1), 0.0).astype(BF16)
    score_a = jnp.where(same_row & upto, dot_nt(c_a, map_a.astype(BF16)), 0.0)
    score_d = jnp.where(same_col & upto, dot_nt(c_d, map_d.astype(BF16)), 0.0)
    weighted[pl.ds(0, count), :] = (values_f * expand(steps, spread_a)).astype(BF16)
    weighted[pl.ds(count, count), :] = (values_f * expand(steps, spread_d)).astype(BF16)
    cum_at = cum_a.T
    cum_dt = cum_d.T
    per_group = LANES // width
    for g in range(inner // LANES):
        total = jnp.zeros((count, LANES), F32)
        for e in range(per_group):
            h = g * per_group + e
            diff_a = cum_a[:, h : h + 1] - cum_at[h : h + 1, :]
            hd = heads + h
            diff_d = cum_d[:, hd : hd + 1] - cum_dt[hd : hd + 1, :]
            mix_a = (jnp.exp(jnp.minimum(diff_a, 0.0)) * score_a).astype(BF16)
            mix_d = (jnp.exp(jnp.minimum(diff_d, 0.0)) * score_d).astype(BF16)
            mix = jnp.concatenate([mix_a, mix_d], axis=1)
            part = dot(mix, weighted[:, g * LANES : (g + 1) * LANES])
            total = jnp.where(lax.div(lane, width) == e, part, total)
        y_ref[:, g * LANES : (g + 1) * LANES] = total

    loads[3].wait()
    column = lax.rem(q, C)
    c_high = pltpu.roll(c_d.astype(F32), state, 1)
    pairs = width * state // LANES
    halves = []
    for c_half in (c_d.astype(F32), c_high):
        half = jnp.zeros((count, pairs * heads), F32)
        for c in range(C):
            rows = jnp.where(column == c, c_half, 0.0).astype(BF16)
            block = jnp.concatenate(
                [top[c, :, n * LANES : (n + 1) * LANES] for n in range(pairs)], axis=0
            )
            half = half + dot_nt(rows, block)
        halves.append(half)
    lane_from = lax.broadcasted_iota(jnp.int32, (inner, inner), 0)
    lane_to = lax.broadcasted_iota(jnp.int32, (inner, inner), 1)
    half_size = pairs * heads
    parity = lax.div(lane_from, half_size)
    pair = lax.div(lax.rem(lane_from, half_size), heads)
    moves = as_mask(lax.rem(lane_from, heads) * width + 2 * pair + parity == lane_to)
    from_top = expand(jnp.concatenate(halves, axis=1), moves)

    def remote(buffer, slot, c_map, first, same, spread, gap):
        block = buffer[slot]
        m = dot(block, wbc[:, first : first + 2 * state]).astype(BF16)
        s = softplus(dot_nt(block, wst[...]) + bias)
        ld = -s * rate
        tail = split_dot(as_mask(same & after), ld)
        whole = split_dot(as_mask(same), ld)
        weight = s * jnp.exp(tail + gap)
        entry = (block.astype(F32) * expand(weight, spread)).astype(BF16)
        score = jnp.where(same, dot_nt(c_map, m), 0.0).astype(BF16)
        acc[...] += dot(score, entry)
        return gap + whole

    acc[...] = jnp.zeros_like(acc)

    def hop_a(t, gap):
        slot = j - 1 - t
        pltpu.make_async_remote_copy(
            src_ref=vals, dst_ref=rva.at[slot], send_sem=as_sem.at[0],
            recv_sem=ar_sem.at[slot], device_id={"cols": slot}, device_id_type=mesh,
        ).wait_recv()
        return remote(rva, slot, c_a, 0, same_row, spread_a, gap)

    lax.fori_loop(0, j, hop_a, jnp.zeros((count, LANES), F32))
    y_ref[...] += expand(jnp.exp(cum_a), spread_a) * acc[...]
    acc[...] = jnp.zeros_like(acc)

    def hop_d(t, gap):
        slot = i - 1 - t
        pltpu.make_async_remote_copy(
            src_ref=vals, dst_ref=rvd.at[slot], send_sem=ds_sem.at[0],
            recv_sem=dr_sem.at[slot], device_id={"rows": slot}, device_id_type=mesh,
        ).wait_recv()
        return remote(rvd, slot, c_d, 2 * state, same_col, spread_d, gap)

    gap_d = lax.fori_loop(0, i, hop_d, jnp.zeros((count, LANES), F32))
    y = (
        y_ref[...]
        + expand(jnp.exp(cum_d), spread_d) * acc[...]
        + expand(jnp.exp(cum_d + gap_d), spread_d) * from_top
        + split_sum(param[0:8, :], spread_a)[2:3, :] * vals[...].astype(F32)
    )
    gated = y * gate[...]
    scale = lax.rsqrt(jnp.mean(gated * gated, axis=-1, keepdims=True) + 1e-05)
    normed = (gated * scale * gain[...]).astype(BF16)
    loads[4].wait()
    out[...] = dot(normed, wout[...]).astype(BF16)

    for k in range(8):
        @pl.when(exists(k))
        def _(k=k):
            halo_copy(k).wait_send()
    for d in range(1, nc):
        @pl.when(j + d < nc)
        def _(d=d):
            send_a(d).wait_send()
    for d in range(1, nr):
        @pl.when(i + d < nr)
        def _(d=d):
            send_d(d).wait_send()


def shards(
    nr, nc,
    tokens, top_state, in_weight, conv_weight, bc_weight, step_weight, step_bias,
    across_rate, down_rate, skip_gain, norm_gain, out_weight,
):
    R, C, model = tokens.shape
    inner = out_weight.shape[0]
    heads = across_rate.shape[0]
    count = R * C
    vmem = pl.BlockSpec(memory_space=pltpu.VMEM)
    result = pl.pallas_call(
        functools.partial(kernel, nr, nc, R, C, heads),
        out_shape=jax.ShapeDtypeStruct((count, model), BF16),
        in_specs=[pl.BlockSpec(memory_space=pltpu.HBM)] * 5 + [vmem] * 7,
        out_specs=vmem,
        scratch_shapes=[
            pltpu.VMEM((count, model), BF16),
            pltpu.VMEM(top_state.shape, BF16),
            pltpu.VMEM(in_weight.shape, BF16),
            pltpu.VMEM(bc_weight.shape, BF16),
            pltpu.VMEM(out_weight.shape, BF16),
            pltpu.VMEM((LANES, inner), BF16),
            pltpu.VMEM((8, LANES), F32),
            pltpu.VMEM((2 * R, model), BF16),
            pltpu.VMEM((8 * STRIP, model), BF16),
            pltpu.VMEM((8 * STRIP, inner), F32),
            pltpu.VMEM((R + 2, 24, inner), F32),
            pltpu.VMEM((count, inner), F32),
            pltpu.VMEM((count, inner), BF16),
            pltpu.VMEM((nc, count, inner), BF16),
            pltpu.VMEM((nr, count, inner), BF16),
            pltpu.VMEM((count, inner), F32),
            pltpu.VMEM((2 * count, inner), BF16),
            pltpu.VMEM((count, inner), F32),
            pltpu.SemaphoreType.DMA((5,)),
            pltpu.SemaphoreType.DMA((8,)),
            pltpu.SemaphoreType.DMA((8,)),
            pltpu.SemaphoreType.DMA((nc,)),
            pltpu.SemaphoreType.DMA((nc,)),
            pltpu.SemaphoreType.DMA((nr,)),
            pltpu.SemaphoreType.DMA((nr,)),
        ],
        compiler_params=pltpu.CompilerParams(
            collective_id=0, has_side_effects=True, vmem_limit_bytes=63 * 1024 * 1024
        ),
    )(
        tokens.reshape(count, model),
        top_state,
        in_weight,
        bc_weight,
        out_weight,
        conv_weight,
        step_weight.T,
        step_bias[None],
        across_rate[None],
        down_rate[None],
        skip_gain[None],
        norm_gain[None],
    )
    return result.reshape(R, C, model)


def solution(mesh):
    in_specs = (
        P(("groups", "rows"), "cols", None),
        P(("groups", "cols"), None, None),
    ) + (P(),) * 10
    out_specs = P(("groups", "rows"), "cols", None)
    return jax.shard_map(
        functools.partial(shards, mesh.shape["rows"], mesh.shape["cols"]),
        mesh=mesh, in_specs=in_specs, out_specs=out_specs, check_vma=False,
    )
```

```python
import functools

import jax
import jax.numpy as jnp
from jax import lax
from jax.experimental import pallas as pl
from jax.experimental.pallas import tpu as pltpu
from jax.sharding import PartitionSpec as P

F32 = jnp.float32
BF16 = jnp.bfloat16
NEIGHBOURS = ((-1, 0), (1, 0), (0, -1), (0, 1), (-1, -1), (-1, 1), (1, -1), (1, 1))
OPPOSITE = (1, 0, 3, 2, 7, 6, 5, 4)
STRIP = 16
LANES = 128


def dot(a, b):
    return jnp.dot(a, b, preferred_element_type=F32)


def dot_nt(a, b):
    return lax.dot_general(a, b, (((1,), (1,)), ((), ())), preferred_element_type=F32)


def split_dot(mask, x):
    high = x.astype(BF16)
    rest = x - high.astype(F32)
    middle = rest.astype(BF16)
    low = (rest - middle.astype(F32)).astype(BF16)
    return dot(mask, high) + dot(mask, middle) + dot(mask, low)


def split_sum(x, mask):
    high = x.astype(BF16)
    rest = x - high.astype(F32)
    middle = rest.astype(BF16)
    low = (rest - middle.astype(F32)).astype(BF16)
    return dot(high, mask) + dot(middle, mask) + dot(low, mask)


def expand(x, spread):
    high = x.astype(BF16)
    low = (x - high.astype(F32)).astype(BF16)
    return dot(high, spread) + dot(low, spread)


def softplus(x):
    return jnp.maximum(x, 0.0) + jnp.log1p(jnp.exp(-jnp.abs(x)))


def silu(x):
    return x / (1.0 + jnp.exp(-x))


def kernel(
    nr, nc, R, C, heads,
    tok_h, top_h, win_h, wbc_h, wout_h, conv, wst_t, step_bias, rate_a, rate_d, skip, gain, out,
    tok, top, win, wbc, wout, wst, param, edge, halo, halo_f, pad, gate, vals, rva, rvd, acc, weighted, y_ref,
    ld_sem, hs_sem, hr_sem, as_sem, ar_sem, ds_sem, dr_sem,
):
    count = R * C
    inner = wout.shape[0]
    state = wbc.shape[1] // 4
    width = inner // heads
    i = lax.axis_index("rows")
    j = lax.axis_index("cols")
    mesh = pl.DeviceIdType.MESH

    def exists(k):
        di, dj = NEIGHBOURS[k]
        a, b = i + di, j + dj
        return (a >= 0) & (a < nr) & (b >= 0) & (b < nc)

    def target(k):
        di, dj = NEIGHBOURS[k]
        return {"rows": i + di, "cols": j + dj}

    loads = [
        pltpu.make_async_copy(a, b, ld_sem.at[n])
        for n, (a, b) in enumerate(
            ((tok_h, tok), (win_h, win), (wbc_h, wbc), (top_h, top), (wout_h, wout))
        )
    ]
    for load in loads:
        load.start()

    barrier = pltpu.get_barrier_semaphore()
    for d in range(1, nc):
        pl.semaphore_signal(
            barrier, inc=1, device_id={"cols": lax.rem(j + d, nc)}, device_id_type=mesh
        )
    for d in range(1, nr):
        pl.semaphore_signal(
            barrier, inc=1, device_id={"rows": lax.rem(i + d, nr)}, device_id_type=mesh
        )
    for k in range(4, 8):
        @pl.when(exists(k))
        def _(k=k):
            pl.semaphore_signal(barrier, inc=1, device_id=target(k), device_id_type=mesh)

    pos = lax.broadcasted_iota(jnp.int32, (2 * R, count), 0)
    src = lax.broadcasted_iota(jnp.int32, (2 * R, count), 1)
    wanted = jnp.where(pos < R, pos * C, (pos - R) * C + C - 1)
    wst[...] = jnp.zeros_like(wst)
    wst[pl.ds(0, 2 * heads), :] = wst_t[...]
    param[...] = jnp.zeros_like(param)
    param[0:1, 0 : 2 * heads] = step_bias[...]
    param[1:2, 0:heads] = rate_a[...]
    param[1:2, heads : 2 * heads] = rate_d[...]
    param[2:3, 0:heads] = skip[...]
    loads[0].wait()
    edge[...] = dot((src == wanted).astype(F32).astype(BF16), tok[...]).astype(BF16)
    corners = sum(jnp.where(exists(k), 1, 0) for k in range(4, 8))
    pl.semaphore_wait(barrier, nc - 1 + nr - 1 + corners)

    def halo_copy(k):
        di, dj = NEIGHBOURS[k]
        if di < 0:
            piece = tok.at[pl.ds(0, STRIP)]
        elif di > 0:
            piece = tok.at[pl.ds(count - STRIP, STRIP)]
        else:
            piece = edge.at[pl.ds(0 if dj < 0 else R, STRIP)]
        return pltpu.make_async_remote_copy(
            src_ref=piece,
            dst_ref=halo.at[pl.ds(OPPOSITE[k] * STRIP, STRIP)],
            send_sem=hs_sem.at[k],
            recv_sem=hr_sem.at[OPPOSITE[k]],
            device_id=target(k),
            device_id_type=mesh,
        )

    for k in range(8):
        @pl.when(exists(k))
        def _(k=k):
            halo_copy(k).start()

        @pl.when(jnp.logical_not(exists(k)))
        def _(k=k):
            halo[pl.ds(k * STRIP, STRIP)] = jnp.zeros((STRIP, halo.shape[1]), BF16)

    loads[1].wait()
    projected = dot(tok[...], win[...])
    gate[...] = silu(projected[:, inner:].astype(BF16).astype(F32))
    mixer = projected[:, :inner].astype(BF16).astype(F32)
    pad[pl.ds(1, R), pl.ds(8, C), :] = mixer.reshape(R, C, inner)

    for k in range(8):
        @pl.when(exists(k))
        def _(k=k):
            pltpu.make_async_remote_copy(
                src_ref=edge.at[pl.ds(0, STRIP)],
                dst_ref=halo.at[pl.ds(k * STRIP, STRIP)],
                send_sem=hs_sem.at[k],
                recv_sem=hr_sem.at[k],
                device_id=target(k),
                device_id_type=mesh,
            ).wait_recv()

    halo_f[...] = dot(halo[...], win[:, :inner]).astype(BF16).astype(F32)

    def halo_rows(k, first, n):
        return halo_f[pl.ds(k * STRIP + first, n), :]

    pad[0, pl.ds(8, C), :] = halo_rows(0, STRIP - C, C)
    pad[R + 1, pl.ds(8, C), :] = halo_rows(1, 0, C)
    for r in range(R):
        pad[1 + r, pl.ds(7, 1), :] = halo_rows(2, r, 1)
        pad[1 + r, pl.ds(8 + C, 1), :] = halo_rows(3, r, 1)
    pad[0, pl.ds(7, 1), :] = halo_rows(4, STRIP - 1, 1)
    pad[0, pl.ds(8 + C, 1), :] = halo_rows(5, STRIP - C, 1)
    pad[R + 1, pl.ds(7, 1), :] = halo_rows(6, C - 1, 1)
    pad[R + 1, pl.ds(8 + C, 1), :] = halo_rows(7, 0, 1)

    summed = jnp.zeros((R, C, inner), F32)
    for b in range(3):
        moved = pad[:, pl.ds(7 + b, C), :]
        for a in range(3):
            tap = conv[pl.ds(3 * a + b, 1), :].reshape(1, 1, inner)
            summed = summed + tap * moved[a : a + R]
    values_f = silu(summed).reshape(count, inner).astype(BF16).astype(F32)
    vals[...] = values_f.astype(BF16)

    def send_a(d):
        return pltpu.make_async_remote_copy(
            src_ref=vals,
            dst_ref=rva.at[j],
            send_sem=as_sem.at[d],
            recv_sem=ar_sem.at[j],
            device_id={"cols": j + d},
            device_id_type=mesh,
        )

    relay = nc >= 4

    def sends_a(d):
        direct = j + d < nc
        return direct & (j != nc - 3) if relay and d == 2 else direct

    def arrival_a(slot):
        return pltpu.make_async_remote_copy(
            src_ref=vals, dst_ref=rva.at[slot], send_sem=as_sem.at[0],
            recv_sem=ar_sem.at[slot], device_id={"cols": slot}, device_id_type=mesh,
        )

    def relayed():
        return pltpu.make_async_remote_copy(
            src_ref=rva.at[nc - 3], dst_ref=rva.at[nc - 3], send_sem=as_sem.at[0],
            recv_sem=ar_sem.at[nc - 3], device_id={"cols": j + 1}, device_id_type=mesh,
        )

    def send_d(d):
        return pltpu.make_async_remote_copy(
            src_ref=vals,
            dst_ref=rvd.at[i],
            send_sem=ds_sem.at[d],
            recv_sem=dr_sem.at[i],
            device_id={"rows": i + d},
            device_id_type=mesh,
        )

    for d in range(1, max(nc, nr)):
        if d < nc:
            @pl.when(sends_a(d))
            def _(d=d):
                send_a(d).start()
        if d < nr:
            @pl.when(i + d < nr)
            def _(d=d):
                send_d(d).start()

    q = lax.broadcasted_iota(jnp.int32, (count, count), 0)
    k_ = lax.broadcasted_iota(jnp.int32, (count, count), 1)
    same_row = lax.div(q, C) == lax.div(k_, C)
    same_col = lax.rem(q, C) == lax.rem(k_, C)
    upto = k_ <= q
    after = k_ > q

    def as_mask(m):
        return jnp.where(m, 1.0, 0.0).astype(BF16)

    lane = lax.broadcasted_iota(jnp.int32, (count, LANES), 1)
    spot = lax.broadcasted_iota(jnp.int32, (LANES, inner), 0)
    head = lax.div(lax.broadcasted_iota(jnp.int32, (LANES, inner), 1), width)
    spread_a = as_mask(spot == head)
    spread_d = as_mask(spot == head + heads)
    bias = param[0:1, :]
    rate = param[1:2, :]

    loads[2].wait()
    maps = dot(vals[...], wbc[...])
    steps = softplus(dot_nt(vals[...], wst[...]) + bias)
    log_decay = -steps * rate
    cum_a = split_dot(as_mask(same_row & upto), log_decay)
    cum_d = split_dot(as_mask(same_col & upto), log_decay)
    map_a = maps[:, : 2 * state]
    map_d = maps[:, 2 * state : 4 * state]
    c_a = jnp.where(lane < state, pltpu.roll(map_a, state, 1), 0.0).astype(BF16)
    c_d = jnp.where(lane < state, pltpu.roll(map_d, state, 1), 0.0).astype(BF16)
    score_a = jnp.where(same_row & upto, dot_nt(c_a, map_a.astype(BF16)), 0.0)
    score_d = jnp.where(same_col & upto, dot_nt(c_d, map_d.astype(BF16)), 0.0)
    weighted[pl.ds(0, count), :] = (values_f * expand(steps, spread_a)).astype(BF16)
    weighted[pl.ds(count, count), :] = (values_f * expand(steps, spread_d)).astype(BF16)
    cum_at = cum_a.T
    cum_dt = cum_d.T
    per_group = LANES // width
    for g in range(inner // LANES):
        total = jnp.zeros((count, LANES), F32)
        for e in range(per_group):
            h = g * per_group + e
            diff_a = cum_a[:, h : h + 1] - cum_at[h : h + 1, :]
            hd = heads + h
            diff_d = cum_d[:, hd : hd + 1] - cum_dt[hd : hd + 1, :]
            mix_a = (jnp.exp(jnp.minimum(diff_a, 0.0)) * score_a).astype(BF16)
            mix_d = (jnp.exp(jnp.minimum(diff_d, 0.0)) * score_d).astype(BF16)
            mix = jnp.concatenate([mix_a, mix_d], axis=1)
            part = dot(mix, weighted[:, g * LANES : (g + 1) * LANES])
            total = jnp.where(lax.div(lane, width) == e, part, total)
        y_ref[:, g * LANES : (g + 1) * LANES] = total

    if relay:
        @pl.when(j == nc - 2)
        def _():
            arrival_a(nc - 3).wait_recv()
            relayed().start()

    loads[3].wait()
    column = lax.rem(q, C)
    c_high = pltpu.roll(c_d.astype(F32), state, 1)
    pairs = width * state // LANES
    halves = []
    for c_half in (c_d.astype(F32), c_high):
        half = jnp.zeros((count, pairs * heads), F32)
        for c in range(C):
            rows = jnp.where(column == c, c_half, 0.0).astype(BF16)
            block = jnp.concatenate(
                [top[c, :, n * LANES : (n + 1) * LANES] for n in range(pairs)], axis=0
            )
            half = half + dot_nt(rows, block)
        halves.append(half)
    lane_from = lax.broadcasted_iota(jnp.int32, (inner, inner), 0)
    lane_to = lax.broadcasted_iota(jnp.int32, (inner, inner), 1)
    half_size = pairs * heads
    parity = lax.div(lane_from, half_size)
    pair = lax.div(lax.rem(lane_from, half_size), heads)
    moves = as_mask(lax.rem(lane_from, heads) * width + 2 * pair + parity == lane_to)
    from_top = expand(jnp.concatenate(halves, axis=1), moves)

    def remote(buffer, slot, c_map, first, same, spread, gap):
        block = buffer[slot]
        m = dot(block, wbc[:, first : first + 2 * state]).astype(BF16)
        s = softplus(dot_nt(block, wst[...]) + bias)
        ld = -s * rate
        tail = split_dot(as_mask(same & after), ld)
        whole = split_dot(as_mask(same), ld)
        weight = s * jnp.exp(tail + gap)
        entry = (block.astype(F32) * expand(weight, spread)).astype(BF16)
        score = jnp.where(same, dot_nt(c_map, m), 0.0).astype(BF16)
        acc[...] += dot(score, entry)
        return gap + whole

    acc[...] = jnp.zeros_like(acc)

    def hop_d(t, gap):
        slot = i - 1 - t
        pltpu.make_async_remote_copy(
            src_ref=vals, dst_ref=rvd.at[slot], send_sem=ds_sem.at[0],
            recv_sem=dr_sem.at[slot], device_id={"rows": slot}, device_id_type=mesh,
        ).wait_recv()
        return remote(rvd, slot, c_d, 2 * state, same_col, spread_d, gap)

    gap_d = lax.fori_loop(0, i, hop_d, jnp.zeros((count, LANES), F32))
    y_ref[...] += (
        expand(jnp.exp(cum_d), spread_d) * acc[...]
        + expand(jnp.exp(cum_d + gap_d), spread_d) * from_top
        + split_sum(param[0:8, :], spread_a)[2:3, :] * vals[...].astype(F32)
    )
    acc[...] = jnp.zeros_like(acc)

    def hop_a(t, gap):
        slot = j - 1 - t
        waits = (j != nc - 2) | (slot != nc - 3) if relay else slot >= 0

        @pl.when(waits)
        def _():
            arrival_a(slot).wait_recv()

        return remote(rva, slot, c_a, 0, same_row, spread_a, gap)

    lax.fori_loop(0, j, hop_a, jnp.zeros((count, LANES), F32))
    y = y_ref[...] + expand(jnp.exp(cum_a), spread_a) * acc[...]
    gated = y * gate[...]
    scale = lax.rsqrt(jnp.mean(gated * gated, axis=-1, keepdims=True) + 1e-05)
    normed = (gated * scale * gain[...]).astype(BF16)
    loads[4].wait()
    out[...] = dot(normed, wout[...]).astype(BF16)

    if relay:
        @pl.when(j == nc - 2)
        def _():
            relayed().wait_send()
    for k in range(8):
        @pl.when(exists(k))
        def _(k=k):
            halo_copy(k).wait_send()
    for d in range(1, nc):
        @pl.when(sends_a(d))
        def _(d=d):
            send_a(d).wait_send()
    for d in range(1, nr):
        @pl.when(i + d < nr)
        def _(d=d):
            send_d(d).wait_send()


def shards(
    nr, nc,
    tokens, top_state, in_weight, conv_weight, bc_weight, step_weight, step_bias,
    across_rate, down_rate, skip_gain, norm_gain, out_weight,
):
    R, C, model = tokens.shape
    inner = out_weight.shape[0]
    heads = across_rate.shape[0]
    count = R * C
    vmem = pl.BlockSpec(memory_space=pltpu.VMEM)
    result = pl.pallas_call(
        functools.partial(kernel, nr, nc, R, C, heads),
        out_shape=jax.ShapeDtypeStruct((count, model), BF16),
        in_specs=[pl.BlockSpec(memory_space=pltpu.HBM)] * 5 + [vmem] * 7,
        out_specs=vmem,
        scratch_shapes=[
            pltpu.VMEM((count, model), BF16),
            pltpu.VMEM(top_state.shape, BF16),
            pltpu.VMEM(in_weight.shape, BF16),
            pltpu.VMEM(bc_weight.shape, BF16),
            pltpu.VMEM(out_weight.shape, BF16),
            pltpu.VMEM((LANES, inner), BF16),
            pltpu.VMEM((8, LANES), F32),
            pltpu.VMEM((2 * R, model), BF16),
            pltpu.VMEM((8 * STRIP, model), BF16),
            pltpu.VMEM((8 * STRIP, inner), F32),
            pltpu.VMEM((R + 2, 24, inner), F32),
            pltpu.VMEM((count, inner), F32),
            pltpu.VMEM((count, inner), BF16),
            pltpu.VMEM((nc, count, inner), BF16),
            pltpu.VMEM((nr, count, inner), BF16),
            pltpu.VMEM((count, inner), F32),
            pltpu.VMEM((2 * count, inner), BF16),
            pltpu.VMEM((count, inner), F32),
            pltpu.SemaphoreType.DMA((5,)),
            pltpu.SemaphoreType.DMA((8,)),
            pltpu.SemaphoreType.DMA((8,)),
            pltpu.SemaphoreType.DMA((nc,)),
            pltpu.SemaphoreType.DMA((nc,)),
            pltpu.SemaphoreType.DMA((nr,)),
            pltpu.SemaphoreType.DMA((nr,)),
        ],
        compiler_params=pltpu.CompilerParams(
            collective_id=0, has_side_effects=True, vmem_limit_bytes=63 * 1024 * 1024
        ),
    )(
        tokens.reshape(count, model),
        top_state,
        in_weight,
        bc_weight,
        out_weight,
        conv_weight,
        step_weight.T,
        step_bias[None],
        across_rate[None],
        down_rate[None],
        skip_gain[None],
        norm_gain[None],
    )
    return result.reshape(R, C, model)


def solution(mesh):
    in_specs = (
        P(("groups", "rows"), "cols", None),
        P(("groups", "cols"), None, None),
    ) + (P(),) * 10
    out_specs = P(("groups", "rows"), "cols", None)
    return jax.shard_map(
        functools.partial(shards, mesh.shape["rows"], mesh.shape["cols"]),
        mesh=mesh, in_specs=in_specs, out_specs=out_specs, check_vma=False,
    )
```

```python
import functools

import jax
import jax.numpy as jnp
from jax import lax
from jax.experimental import pallas as pl
from jax.experimental.pallas import tpu as pltpu
from jax.sharding import PartitionSpec as P

F32 = jnp.float32
BF16 = jnp.bfloat16
NEIGHBOURS = ((-1, 0), (1, 0), (0, -1), (0, 1), (-1, -1), (-1, 1), (1, -1), (1, 1))
OPPOSITE = (1, 0, 3, 2, 7, 6, 5, 4)
STRIP = 16
LANES = 128


def dot(a, b):
    return jnp.dot(a, b, preferred_element_type=F32)


def dot_nt(a, b):
    return lax.dot_general(a, b, (((1,), (1,)), ((), ())), preferred_element_type=F32)


def split_dot(mask, x):
    high = x.astype(BF16)
    rest = x - high.astype(F32)
    middle = rest.astype(BF16)
    low = (rest - middle.astype(F32)).astype(BF16)
    return dot(mask, high) + dot(mask, middle) + dot(mask, low)


def split_sum(x, mask):
    high = x.astype(BF16)
    rest = x - high.astype(F32)
    middle = rest.astype(BF16)
    low = (rest - middle.astype(F32)).astype(BF16)
    return dot(high, mask) + dot(middle, mask) + dot(low, mask)


def expand(x, spread):
    high = x.astype(BF16)
    low = (x - high.astype(F32)).astype(BF16)
    return dot(high, spread) + dot(low, spread)


def softplus(x):
    return jnp.maximum(x, 0.0) + jnp.log1p(jnp.exp(-jnp.abs(x)))


def silu(x):
    return x / (1.0 + jnp.exp(-x))


def kernel(
    nr, nc, R, C, heads,
    tok_h, top_h, win_h, wbc_h, wout_h, conv, wst_t, step_bias, rate_a, rate_d, skip, gain, out,
    tok, top, win, wbc, wout, wst, param, edge, halo, halo_f, pad, gate, vals, rva, rvd, acc, weighted, y_ref,
    ld_sem, hs_sem, hr_sem, as_sem, ar_sem, ds_sem, dr_sem,
):
    count = R * C
    inner = wout.shape[0]
    state = wbc.shape[1] // 4
    width = inner // heads
    i = lax.axis_index("rows")
    j = lax.axis_index("cols")
    mesh = pl.DeviceIdType.MESH

    def exists(k):
        di, dj = NEIGHBOURS[k]
        a, b = i + di, j + dj
        return (a >= 0) & (a < nr) & (b >= 0) & (b < nc)

    def target(k):
        di, dj = NEIGHBOURS[k]
        return {"rows": i + di, "cols": j + dj}

    loads = [
        pltpu.make_async_copy(a, b, ld_sem.at[n])
        for n, (a, b) in enumerate(
            ((tok_h, tok), (win_h, win), (wbc_h, wbc), (top_h, top), (wout_h, wout))
        )
    ]
    for load in loads:
        load.start()

    barrier = pltpu.get_barrier_semaphore()
    for d in range(1, nc):
        pl.semaphore_signal(
            barrier, inc=1, device_id={"cols": lax.rem(j + d, nc)}, device_id_type=mesh
        )
    for d in range(1, nr):
        pl.semaphore_signal(
            barrier, inc=1, device_id={"rows": lax.rem(i + d, nr)}, device_id_type=mesh
        )
    for k in range(4, 8):
        @pl.when(exists(k))
        def _(k=k):
            pl.semaphore_signal(barrier, inc=1, device_id=target(k), device_id_type=mesh)

    pos = lax.broadcasted_iota(jnp.int32, (2 * R, count), 0)
    src = lax.broadcasted_iota(jnp.int32, (2 * R, count), 1)
    wanted = jnp.where(pos < R, pos * C, (pos - R) * C + C - 1)
    wst[...] = jnp.zeros_like(wst)
    wst[pl.ds(0, 2 * heads), :] = wst_t[...]
    param[...] = jnp.zeros_like(param)
    param[0:1, 0 : 2 * heads] = step_bias[...]
    param[1:2, 0:heads] = rate_a[...]
    param[1:2, heads : 2 * heads] = rate_d[...]
    param[2:3, 0:heads] = skip[...]
    loads[0].wait()
    edge[...] = dot((src == wanted).astype(F32).astype(BF16), tok[...]).astype(BF16)
    corners = sum(jnp.where(exists(k), 1, 0) for k in range(4, 8))
    pl.semaphore_wait(barrier, nc - 1 + nr - 1 + corners)

    def halo_copy(k):
        di, dj = NEIGHBOURS[k]
        if di < 0:
            piece = tok.at[pl.ds(0, STRIP)]
        elif di > 0:
            piece = tok.at[pl.ds(count - STRIP, STRIP)]
        else:
            piece = edge.at[pl.ds(0 if dj < 0 else R, STRIP)]
        return pltpu.make_async_remote_copy(
            src_ref=piece,
            dst_ref=halo.at[pl.ds(OPPOSITE[k] * STRIP, STRIP)],
            send_sem=hs_sem.at[k],
            recv_sem=hr_sem.at[OPPOSITE[k]],
            device_id=target(k),
            device_id_type=mesh,
        )

    for k in range(8):
        @pl.when(exists(k))
        def _(k=k):
            halo_copy(k).start()

        @pl.when(jnp.logical_not(exists(k)))
        def _(k=k):
            halo[pl.ds(k * STRIP, STRIP)] = jnp.zeros((STRIP, halo.shape[1]), BF16)

    loads[1].wait()
    projected = dot(tok[...], win[...])
    gate[...] = silu(projected[:, inner:].astype(BF16).astype(F32))
    mixer = projected[:, :inner].astype(BF16).astype(F32)
    pad[pl.ds(1, R), pl.ds(8, C), :] = mixer.reshape(R, C, inner)

    for k in range(8):
        @pl.when(exists(k))
        def _(k=k):
            pltpu.make_async_remote_copy(
                src_ref=edge.at[pl.ds(0, STRIP)],
                dst_ref=halo.at[pl.ds(k * STRIP, STRIP)],
                send_sem=hs_sem.at[k],
                recv_sem=hr_sem.at[k],
                device_id=target(k),
                device_id_type=mesh,
            ).wait_recv()

    halo_f[...] = dot(halo[...], win[:, :inner]).astype(BF16).astype(F32)

    def halo_rows(k, first, n):
        return halo_f[pl.ds(k * STRIP + first, n), :]

    pad[0, pl.ds(8, C), :] = halo_rows(0, STRIP - C, C)
    pad[R + 1, pl.ds(8, C), :] = halo_rows(1, 0, C)
    for r in range(R):
        pad[1 + r, pl.ds(7, 1), :] = halo_rows(2, r, 1)
        pad[1 + r, pl.ds(8 + C, 1), :] = halo_rows(3, r, 1)
    pad[0, pl.ds(7, 1), :] = halo_rows(4, STRIP - 1, 1)
    pad[0, pl.ds(8 + C, 1), :] = halo_rows(5, STRIP - C, 1)
    pad[R + 1, pl.ds(7, 1), :] = halo_rows(6, C - 1, 1)
    pad[R + 1, pl.ds(8 + C, 1), :] = halo_rows(7, 0, 1)

    summed = jnp.zeros((R, C, inner), F32)
    for b in range(3):
        moved = pad[:, pl.ds(7 + b, C), :]
        for a in range(3):
            tap = conv[pl.ds(3 * a + b, 1), :].reshape(1, 1, inner)
            summed = summed + tap * moved[a : a + R]
    values_f = silu(summed).reshape(count, inner).astype(BF16).astype(F32)
    vals[...] = values_f.astype(BF16)

    def send_a(d):
        return pltpu.make_async_remote_copy(
            src_ref=vals,
            dst_ref=rva.at[j],
            send_sem=as_sem.at[d],
            recv_sem=ar_sem.at[j],
            device_id={"cols": j + d},
            device_id_type=mesh,
        )

    relay = nc >= 4

    def sends_a(d):
        direct = j + d < nc
        return direct & (j != nc - 3) if relay and d == 2 else direct

    def arrival_a(slot):
        return pltpu.make_async_remote_copy(
            src_ref=vals, dst_ref=rva.at[slot], send_sem=as_sem.at[0],
            recv_sem=ar_sem.at[slot], device_id={"cols": slot}, device_id_type=mesh,
        )

    def relayed():
        return pltpu.make_async_remote_copy(
            src_ref=rva.at[nc - 3], dst_ref=rva.at[nc - 3], send_sem=as_sem.at[0],
            recv_sem=ar_sem.at[nc - 3], device_id={"cols": j + 1}, device_id_type=mesh,
        )

    def send_d(d):
        return pltpu.make_async_remote_copy(
            src_ref=vals,
            dst_ref=rvd.at[i],
            send_sem=ds_sem.at[d],
            recv_sem=dr_sem.at[i],
            device_id={"rows": i + d},
            device_id_type=mesh,
        )

    for d in range(1, max(nc, nr)):
        if d < nc:
            if d == 1:
                @pl.when(sends_a(d))
                def _(d=d):
                    send_a(d).start()
        if d == 1:
            @pl.when(i + d < nr)
            def _(d=d):
                send_d(d).start()

    q = lax.broadcasted_iota(jnp.int32, (count, count), 0)
    k_ = lax.broadcasted_iota(jnp.int32, (count, count), 1)
    same_row = lax.div(q, C) == lax.div(k_, C)
    same_col = lax.rem(q, C) == lax.rem(k_, C)
    upto = k_ <= q
    after = k_ > q

    def as_mask(m):
        return jnp.where(m, 1.0, 0.0).astype(BF16)

    lane = lax.broadcasted_iota(jnp.int32, (count, LANES), 1)
    spot = lax.broadcasted_iota(jnp.int32, (LANES, inner), 0)
    head = lax.div(lax.broadcasted_iota(jnp.int32, (LANES, inner), 1), width)
    spread_a = as_mask(spot == head)
    spread_d = as_mask(spot == head + heads)
    bias = param[0:1, :]
    rate = param[1:2, :]

    loads[2].wait()
    maps = dot(vals[...], wbc[...])
    steps = softplus(dot_nt(vals[...], wst[...]) + bias)
    log_decay = -steps * rate
    cum_a = split_dot(as_mask(same_row & upto), log_decay)
    cum_d = split_dot(as_mask(same_col & upto), log_decay)
    map_a = maps[:, : 2 * state]
    map_d = maps[:, 2 * state : 4 * state]
    c_a = jnp.where(lane < state, pltpu.roll(map_a, state, 1), 0.0).astype(BF16)
    c_d = jnp.where(lane < state, pltpu.roll(map_d, state, 1), 0.0).astype(BF16)
    score_a = jnp.where(same_row & upto, dot_nt(c_a, map_a.astype(BF16)), 0.0)
    score_d = jnp.where(same_col & upto, dot_nt(c_d, map_d.astype(BF16)), 0.0)
    weighted[pl.ds(0, count), :] = (values_f * expand(steps, spread_a)).astype(BF16)
    weighted[pl.ds(count, count), :] = (values_f * expand(steps, spread_d)).astype(BF16)
    cum_at = cum_a.T
    cum_dt = cum_d.T
    per_group = LANES // width
    for g in range(inner // LANES):
        total = jnp.zeros((count, LANES), F32)
        for e in range(per_group):
            h = g * per_group + e
            diff_a = cum_a[:, h : h + 1] - cum_at[h : h + 1, :]
            hd = heads + h
            diff_d = cum_d[:, hd : hd + 1] - cum_dt[hd : hd + 1, :]
            mix_a = (jnp.exp(jnp.minimum(diff_a, 0.0)) * score_a).astype(BF16)
            mix_d = (jnp.exp(jnp.minimum(diff_d, 0.0)) * score_d).astype(BF16)
            mix = jnp.concatenate([mix_a, mix_d], axis=1)
            part = dot(mix, weighted[:, g * LANES : (g + 1) * LANES])
            total = jnp.where(lax.div(lane, width) == e, part, total)
        y_ref[:, g * LANES : (g + 1) * LANES] = total

    for d in range(nc - 1, 1, -1):
        @pl.when(sends_a(d))
        def _(d=d):
            send_a(d).start()

    for d in range(nr - 1, 1, -1):
        @pl.when(i + d < nr)
        def _(d=d):
            send_d(d).start()

    if relay:
        @pl.when(j == nc - 2)
        def _():
            arrival_a(nc - 3).wait_recv()
            relayed().start()

    loads[3].wait()
    column = lax.rem(q, C)
    c_high = pltpu.roll(c_d.astype(F32), state, 1)
    pairs = width * state // LANES
    halves = []
    for c_half in (c_d.astype(F32), c_high):
        half = jnp.zeros((count, pairs * heads), F32)
        for c in range(C):
            rows = jnp.where(column == c, c_half, 0.0).astype(BF16)
            block = jnp.concatenate(
                [top[c, :, n * LANES : (n + 1) * LANES] for n in range(pairs)], axis=0
            )
            half = half + dot_nt(rows, block)
        halves.append(half)
    lane_from = lax.broadcasted_iota(jnp.int32, (inner, inner), 0)
    lane_to = lax.broadcasted_iota(jnp.int32, (inner, inner), 1)
    half_size = pairs * heads
    parity = lax.div(lane_from, half_size)
    pair = lax.div(lax.rem(lane_from, half_size), heads)
    moves = as_mask(lax.rem(lane_from, heads) * width + 2 * pair + parity == lane_to)
    from_top = expand(jnp.concatenate(halves, axis=1), moves)

    def remote(buffer, slot, c_map, first, same, spread, gap):
        block = buffer[slot]
        m = dot(block, wbc[:, first : first + 2 * state]).astype(BF16)
        s = softplus(dot_nt(block, wst[...]) + bias)
        ld = -s * rate
        tail = split_dot(as_mask(same & after), ld)
        whole = split_dot(as_mask(same), ld)
        weight = s * jnp.exp(tail + gap)
        entry = (block.astype(F32) * expand(weight, spread)).astype(BF16)
        score = jnp.where(same, dot_nt(c_map, m), 0.0).astype(BF16)
        acc[...] += dot(score, entry)
        return gap + whole

    acc[...] = jnp.zeros_like(acc)

    def hop_d(t, gap):
        slot = i - 1 - t
        pltpu.make_async_remote_copy(
            src_ref=vals, dst_ref=rvd.at[slot], send_sem=ds_sem.at[0],
            recv_sem=dr_sem.at[slot], device_id={"rows": slot}, device_id_type=mesh,
        ).wait_recv()
        return remote(rvd, slot, c_d, 2 * state, same_col, spread_d, gap)

    gap_d = lax.fori_loop(0, i, hop_d, jnp.zeros((count, LANES), F32))
    y_ref[...] += (
        expand(jnp.exp(cum_d), spread_d) * acc[...]
        + expand(jnp.exp(cum_d + gap_d), spread_d) * from_top
        + split_sum(param[0:8, :], spread_a)[2:3, :] * vals[...].astype(F32)
    )
    acc[...] = jnp.zeros_like(acc)

    def hop_a(t, gap):
        slot = j - 1 - t
        waits = (j != nc - 2) | (slot != nc - 3) if relay else slot >= 0

        @pl.when(waits)
        def _():
            arrival_a(slot).wait_recv()

        return remote(rva, slot, c_a, 0, same_row, spread_a, gap)

    lax.fori_loop(0, j, hop_a, jnp.zeros((count, LANES), F32))
    y = y_ref[...] + expand(jnp.exp(cum_a), spread_a) * acc[...]
    gated = y * gate[...]
    scale = lax.rsqrt(jnp.mean(gated * gated, axis=-1, keepdims=True) + 1e-05)
    normed = (gated * scale * gain[...]).astype(BF16)
    loads[4].wait()
    out[...] = dot(normed, wout[...]).astype(BF16)

    if relay:
        @pl.when(j == nc - 2)
        def _():
            relayed().wait_send()
    for k in range(8):
        @pl.when(exists(k))
        def _(k=k):
            halo_copy(k).wait_send()
    for d in range(1, nc):
        @pl.when(sends_a(d))
        def _(d=d):
            send_a(d).wait_send()
    for d in range(1, nr):
        @pl.when(i + d < nr)
        def _(d=d):
            send_d(d).wait_send()


def shards(
    nr, nc,
    tokens, top_state, in_weight, conv_weight, bc_weight, step_weight, step_bias,
    across_rate, down_rate, skip_gain, norm_gain, out_weight,
):
    R, C, model = tokens.shape
    inner = out_weight.shape[0]
    heads = across_rate.shape[0]
    count = R * C
    vmem = pl.BlockSpec(memory_space=pltpu.VMEM)
    result = pl.pallas_call(
        functools.partial(kernel, nr, nc, R, C, heads),
        out_shape=jax.ShapeDtypeStruct((count, model), BF16),
        in_specs=[pl.BlockSpec(memory_space=pltpu.HBM)] * 5 + [vmem] * 7,
        out_specs=vmem,
        scratch_shapes=[
            pltpu.VMEM((count, model), BF16),
            pltpu.VMEM(top_state.shape, BF16),
            pltpu.VMEM(in_weight.shape, BF16),
            pltpu.VMEM(bc_weight.shape, BF16),
            pltpu.VMEM(out_weight.shape, BF16),
            pltpu.VMEM((LANES, inner), BF16),
            pltpu.VMEM((8, LANES), F32),
            pltpu.VMEM((2 * R, model), BF16),
            pltpu.VMEM((8 * STRIP, model), BF16),
            pltpu.VMEM((8 * STRIP, inner), F32),
            pltpu.VMEM((R + 2, 24, inner), F32),
            pltpu.VMEM((count, inner), F32),
            pltpu.VMEM((count, inner), BF16),
            pltpu.VMEM((nc, count, inner), BF16),
            pltpu.VMEM((nr, count, inner), BF16),
            pltpu.VMEM((count, inner), F32),
            pltpu.VMEM((2 * count, inner), BF16),
            pltpu.VMEM((count, inner), F32),
            pltpu.SemaphoreType.DMA((5,)),
            pltpu.SemaphoreType.DMA((8,)),
            pltpu.SemaphoreType.DMA((8,)),
            pltpu.SemaphoreType.DMA((nc,)),
            pltpu.SemaphoreType.DMA((nc,)),
            pltpu.SemaphoreType.DMA((nr,)),
            pltpu.SemaphoreType.DMA((nr,)),
        ],
        compiler_params=pltpu.CompilerParams(
            collective_id=0, has_side_effects=True, vmem_limit_bytes=55000 * 1024
        ),
    )(
        tokens.reshape(count, model),
        top_state,
        in_weight,
        bc_weight,
        out_weight,
        conv_weight,
        step_weight.T,
        step_bias[None],
        across_rate[None],
        down_rate[None],
        skip_gain[None],
        norm_gain[None],
    )
    return result.reshape(R, C, model)


def solution(mesh):
    in_specs = (
        P(("groups", "rows"), "cols", None),
        P(("groups", "cols"), None, None),
    ) + (P(),) * 10
    out_specs = P(("groups", "rows"), "cols", None)
    return jax.shard_map(
        functools.partial(shards, mesh.shape["rows"], mesh.shape["cols"]),
        mesh=mesh, in_specs=in_specs, out_specs=out_specs, check_vma=False,
    )
```
